32 devices in a mesh: prow: 8 (over z, core), pcol: 4 (over y, x).
Axes of the slice: x: 2, y: 2, z: 4, core: 2. Of those that a mesh axis runs over, the one named last changes fastest.
Arguments:
- trailing_in: float32 [2048, 2048], P('prow', 'pcol'), may hold values from -6 to 6
- panel_t: float32 [256, 2048], P('pcol', 'prow'), may hold values from -0.375 to 0.375
- pivots: int32 [256], replicated, may hold values from 0 to 2047, as said below
Outputs:
- trailing: float32 [2048, 2048], P('prow', 'pcol')
The draws below stay inside these ranges and needn't reach their ends.
Inputs may be any that keep to these rules, and one draw needn't show every extreme that they name: pivots[k] is at least k and below 2048; one entry equals 2047.
All inputs are finite; a program needn't handle non-finite values.
Results may differ from the reference program's by a relative error of at most 0.000076.
Values sent between devices are 32-bit elements; how exact they have to be, the bound alone decides.
No kernel may reach another device: no remote copies, remote signals or barrier semaphores. Data moves between devices by JAX's collectives and lax.ppermute only.
A program may use at most 64 MiB of HBM per device.

```python
import jax
import jax.numpy as jnp
from jax import lax

NB = 256
M = 2048
NC = 2048


def draw_pivots(key, part):
    steps = jnp.arange(NB, dtype=jnp.int32)
    raw = jax.random.randint(key, (NB,), 0, M, dtype=jnp.int32)
    chosen = steps + raw % (M - steps)
    where_last = jax.random.randint(jax.random.fold_in(key, 7), (), 0, NB, dtype=jnp.int32)
    return jnp.where(steps == where_last, M - 1, chosen).astype(jnp.int32)


def shard_levels(key, dims, cuts, smallest, high):
    gain = 1.0
    for position, blocks in cuts:
        draws = jax.random.uniform(jax.random.fold_in(jax.random.fold_in(key, 6), position), (blocks,), jnp.float32, smallest / len(cuts), high / len(cuts))
        gain = gain * jnp.repeat(jnp.exp(draws), dims[position] // blocks).reshape((-1,) + (1,) * (len(dims) - 1 - position))
    return gain


def gaussian(rng, extent, deviation, bound, pieces=(), kind=jnp.bfloat16):
    loudness = shard_levels(rng, extent, pieces, -0.22, 0.18) if pieces else 1.0
    drawn = jax.random.normal(rng, extent, jnp.float32) * deviation * loudness
    return jnp.minimum(jnp.maximum(drawn, -bound), bound).astype(kind)


def setup_inputs(seed: int = 0) -> dict:
    keys = jax.random.split(jax.random.key(seed), 4)
    trailing_in = gaussian(keys[0], (M, NC), 1.0, 6.0, ((0, 8), (1, 4)), jnp.float32)
    panel_t = gaussian(keys[1], (NB, M), NB ** -0.5, 0.375, ((0, 4), (1, 8)), jnp.float32)
    pivots = draw_pivots(jax.random.fold_in(keys[3], 71), 0)
    return dict(trailing_in=trailing_in, panel_t=panel_t, pivots=pivots)


def reference(trailing_in, panel_t, pivots):

    def exchange_one(k, perm):
        target = pivots[k]
        first = perm[k]
        second = perm[target]
        return perm.at[k].set(second).at[target].set(first)
    perm = lax.fori_loop(0, NB, exchange_one, jnp.arange(M, dtype=jnp.int32))
    moved = trailing_in[perm]
    lower = panel_t.T
    upper = jax.scipy.linalg.solve_triangular(lower[:NB], moved[:NB], lower=True, unit_diagonal=True)
    update = jnp.dot(lower.astype(jnp.float32), upper.astype(jnp.float32), precision=lax.Precision.HIGHEST, preferred_element_type=jnp.float32)
    result = moved - update
    return result.at[:NB].set(upper)
```

```python
import functools

import jax
import jax.numpy as jnp
from jax import lax
from jax.experimental import pallas as pl
from jax.experimental.pallas import tpu as pltpu
from jax.sharding import PartitionSpec as P

VMEM = pl.BlockSpec(memory_space=pltpu.VMEM)
SMEM = pl.BlockSpec(memory_space=pltpu.SMEM)
ANY = pl.BlockSpec(memory_space=pl.ANY)
F32 = jnp.float32
UNROLL = 32


def pair_exchange(value, axis, bit):
    size = lax.axis_size(axis)
    return lax.ppermute(value, axis, [(i, i ^ bit) for i in range(size)])


def inside(rows, low, count):
    return (rows >= low) & (rows < low + count)


def pick_body(pivots, trailing, keep, send, slots, table, block, sem):
    width = pivots.shape[0]
    rows = trailing.shape[0]
    half = width // 2
    me = lax.axis_index("prow")
    core = lax.rem(me, 2)
    first = me * rows
    load = pltpu.make_async_copy(trailing, block, sem)
    load.start()

    def fill(i, _):
        for u in range(UNROLL):
            table[i * UNROLL + u] = i * UNROLL + u
        for u in range(UNROLL):
            pivot = pivots[i * UNROLL + u]
            table[pivot] = pivot
        return 0

    def exchange(i, _):
        for u in range(UNROLL):
            k = i * UNROLL + u
            pivot = pivots[k]
            mine = table[k]
            slots[k] = table[pivot]
            table[pivot] = mine
        return 0

    lax.fori_loop(0, width // UNROLL, fill, 0)
    lax.fori_loop(0, width // UNROLL, exchange, 0)
    load.wait()

    def pick(offset, target):
        def some(i, _):
            for u in range(UNROLL):
                j = i * UNROLL + u
                row = slots[offset + j]
                local = row - first
                own = (local >= 0) & (local < rows)
                index = jnp.where(own, local, jnp.where(me == 0, table[row], 0))
                target[pl.ds(j, 1), :] = block[pl.ds(index, 1), :]
            return 0

        lax.fori_loop(0, half // UNROLL, some, 0)

    pick((1 - core) * half, send)
    pick(core * half, keep)


def column_body(slots, column):
    def some(i, _):
        for u in range(UNROLL):
            j = i * UNROLL + u
            column[pl.ds(j, 1), :] = jnp.full((1, column.shape[1]), slots[j], jnp.int32)
        return 0

    lax.fori_loop(0, column.shape[0] // UNROLL, some, 0)


def chip_body(rows, keep, recv, column, *pieces):
    me = lax.axis_index("prow")
    chip, core = me // 2, lax.rem(me, 2)
    for d, piece in enumerate(pieces):
        part = lax.bitwise_xor(chip, d)
        ids = column[core * len(pieces) + part][:, 0:1]
        second = inside(ids, (2 * chip + 1) * rows, rows)
        piece[...] = jnp.where(second == (core == 1), keep[part], recv[part])


def owner_body(rows, count, column, *refs):
    pieces, outs = refs[:count], refs[count:]
    me = lax.axis_index("prow")
    chip, core = me // 2, lax.rem(me, 2)
    ids = column[core * count + chip][:, 0:1]
    holds = [inside(ids, lax.bitwise_xor(chip, d) * 2 * rows, 2 * rows) for d in range(count)]
    chosen = pieces[0][...]
    leaving = pieces[0][...]
    for d in range(1, count):
        value = pieces[d][...]
        chosen = jnp.where(holds[d], value, chosen)
        leaving = jnp.where(chip == d, value, leaving)
    for d in range(count):
        outs[d][...] = jnp.where(holds[d], leaving, chosen)


def share_body(rows, keep, recv, column, *refs):
    count = keep.shape[0]
    parts, (own, send) = refs[:count], refs[count:]
    me = lax.axis_index("prow")
    chip, core = me // 2, lax.rem(me, 2)
    for d in range(count):
        part = lax.bitwise_xor(chip, d)
        ids = column[core * count + part][:, 0:1]
        mine, theirs = keep[part], recv[part]
        second = inside(ids, (2 * chip + 1) * rows, rows)
        here = jnp.where(second == (core == 1), mine, theirs)
        there = jnp.where(second & (chip == 0), jnp.where(core == 0, mine, theirs), parts[d][...])
        own[part] = jnp.where(inside(ids, lax.bitwise_xor(me, 1) * rows, rows), here, there)
        send[part] = jnp.where(inside(ids, me * rows, rows), here, there)


def dot(a, b):
    return lax.dot(a, b, precision=lax.Precision.HIGHEST, preferred_element_type=F32)


def factor_body(count, column, trailing, *refs):
    diag, lower = refs[:count], refs[count : 2 * count]
    a_ref, sel_ref, base_ref, diag_t, lower_t = refs[2 * count :]
    depth = diag[0].shape[0]
    width = depth * count
    rows = trailing.shape[0]
    me = lax.axis_index("prow")
    mine = lax.axis_index("pcol")
    for d in range(count):
        at = pl.ds(pl.multiple_of(lax.bitwise_xor(mine, d) * depth, depth), depth)
        diag_t[at, :] = diag[d][...]
        lower_t[at, :] = lower[d][...]
    i = lax.broadcasted_iota(jnp.int32, (width, width), 0)
    j = lax.broadcasted_iota(jnp.int32, (width, width), 1)
    full = diag_t[...]
    inverse = (i == j).astype(F32)
    size = 1
    while size < width:
        cross = (i // size + 1 == j // size) & (lax.rem(i // size, 2) == 0)
        block = jnp.where(cross, full, 0.0)
        inverse = inverse - (block if size == 1 else dot(inverse, dot(block, inverse)))
        size *= 2
    minus = -dot(inverse, lower_t[...])
    a_ref[...] = jnp.where(me == 0, inverse, minus).T
    ids = column[...].astype(F32).T[0:1, :]
    own = (me * rows + lax.broadcasted_iota(jnp.int32, (rows, width), 0)).astype(F32)
    match = (ids == own) & (me > 0)
    sel = jnp.where(match, 1.0, 0.0)
    sel_ref[...] = sel.astype(jnp.bfloat16)
    drop = (jnp.max(sel, axis=1, keepdims=True) > 0.0) | (me == 0)
    base_ref[...] = jnp.where(drop, 0.0, trailing[...])


def finish_body(rows, column, keep, send, own, recv, a_ref, sel_ref, base, out):
    half = keep.shape[0]
    me = lax.axis_index("prow")
    core = lax.rem(me, 2)

    def part(start, picked, arrived):
        at = pl.ds(pl.multiple_of(start, half), half)
        ids = column[at, 0:1]
        value = arrived[...]
        chosen = jnp.where(inside(ids, me * rows, rows), picked[...], value)
        high = value.astype(jnp.bfloat16)
        rest = value - high.astype(F32)
        middle = rest.astype(jnp.bfloat16)
        low = (rest - middle.astype(F32)).astype(jnp.bfloat16)
        sel = sel_ref[:, at]
        total = dot(a_ref[:, at], chosen)
        for term in (low, middle, high):
            total += lax.dot(sel, term, preferred_element_type=F32)
        return total

    first = part(core * half, keep, own)
    out[...] = base[...] + first + part((1 - core) * half, send, recv)


def on_device(trailing_in, panel_t, pivots):
    rows, cols = trailing_in.shape
    width = pivots.shape[0]
    half = width // 2
    devices = lax.axis_size("prow")
    chips = devices // 2
    spread = lax.axis_size("pcol")
    size = half // chips
    depth = panel_t.shape[0]
    assert rows == width and size * chips == half and depth * spread == width

    def array(*shape, dtype=F32):
        return jax.ShapeDtypeStruct(shape, dtype)

    me = lax.axis_index("prow")
    diag = panel_t
    bit = devices // 2
    while bit:
        diag = jnp.where((me & bit) > 0, pair_exchange(diag, "prow", bit), diag)
        bit //= 2
    lowers = [panel_t] + [pair_exchange(panel_t, "pcol", d) for d in range(1, spread)]
    diags = [diag] + [pair_exchange(diag, "pcol", d) for d in range(1, spread)]

    keep, send, slots = pl.pallas_call(
        pick_body,
        out_shape=(array(half, cols), array(half, cols), array(width, dtype=jnp.int32)),
        in_specs=[SMEM, ANY],
        out_specs=(VMEM, VMEM, SMEM),
        scratch_shapes=[
            pltpu.SMEM((rows * devices,), jnp.int32),
            pltpu.VMEM((rows, cols), F32),
            pltpu.SemaphoreType.DMA,
        ],
        name="pick",
    )(pivots, trailing_in)
    column = pl.pallas_call(
        column_body,
        out_shape=array(width, 128, dtype=jnp.int32),
        in_specs=[SMEM],
        out_specs=VMEM,
        name="column",
    )(slots)
    recv = pair_exchange(send, "prow", 1).reshape(chips, size, cols)
    cut = keep.reshape(chips, size, cols)
    ids = column.reshape(devices, size, 128)
    pieces = pl.pallas_call(
        functools.partial(chip_body, rows),
        out_shape=[array(size, cols)] * chips,
        in_specs=[VMEM] * 3,
        out_specs=[VMEM] * chips,
        name="chip",
    )(cut, recv, ids)
    gathered = [pieces[0]] + [pair_exchange(pieces[d], "prow", 2 * d) for d in range(1, chips)]
    parts = pl.pallas_call(
        functools.partial(owner_body, rows, chips),
        out_shape=[array(size, cols)] * chips,
        in_specs=[VMEM] * (1 + chips),
        out_specs=[VMEM] * chips,
        name="owner",
    )(ids, *gathered)
    parts = [parts[0]] + [pair_exchange(parts[d], "prow", 2 * d) for d in range(1, chips)]
    own, other = pl.pallas_call(
        functools.partial(share_body, rows),
        out_shape=[array(chips, size, cols)] * 2,
        in_specs=[VMEM] * (3 + chips),
        out_specs=[VMEM] * 2,
        name="share",
    )(cut, recv, ids, *parts)
    own = own.reshape(half, cols)
    arrived = pair_exchange(other, "prow", 1).reshape(half, cols)
    a, sel, base = pl.pallas_call(
        functools.partial(factor_body, spread),
        out_shape=(array(rows, width), array(rows, width, dtype=jnp.bfloat16), array(rows, cols)),
        in_specs=[VMEM] * (2 + 2 * spread),
        out_specs=(VMEM,) * 3,
        scratch_shapes=[pltpu.VMEM((width, width), F32), pltpu.VMEM((width, rows), F32)],
        name="factor",
    )(column, trailing_in, *diags, *lowers)
    return pl.pallas_call(
        functools.partial(finish_body, rows),
        out_shape=array(rows, cols),
        in_specs=[VMEM] * 8,
        out_specs=VMEM,
        name="finish",
    )(column, keep, send, own, arrived, a, sel, base)


def solution(mesh):
    in_specs = (P("prow", "pcol"), P("pcol", "prow"), P())
    out_specs = P("prow", "pcol")
    return jax.shard_map(
        on_device, mesh=mesh, in_specs=in_specs, out_specs=out_specs, check_vma=False
    )
```

```python
import functools

import jax
import jax.numpy as jnp
from jax import lax
from jax.experimental import pallas as pl
from jax.experimental.pallas import tpu as pltpu
from jax.sharding import PartitionSpec as P

VMEM = pl.BlockSpec(memory_space=pltpu.VMEM)
HBM = pl.BlockSpec(memory_space=pltpu.HBM)
F32 = jnp.float32
UNROLL = 32
VMEM_LIMIT = 16 << 20


def pair_exchange(value, axis, bit):
    size = lax.axis_size(axis)
    return lax.ppermute(value, axis, [(i, i ^ bit) for i in range(size)])


def call(body, outs, *args, in_specs=None, out_specs=None, scratch=()):
    if in_specs is None:
        in_specs = [VMEM] * len(args)
    placed = [
        pltpu.with_memory_space_constraint(arg, spec.memory_space)
        for arg, spec in zip(args, in_specs)
    ]
    return kernel(body, outs, placed, in_specs, out_specs, scratch)


def kernel(body, outs, placed, in_specs, out_specs, scratch):
    return pl.pallas_call(
        body,
        out_shape=tuple(outs),
        in_specs=list(in_specs),
        out_specs=tuple(out_specs) if out_specs else (VMEM,) * len(outs),
        scratch_shapes=list(scratch),
        compiler_params=pltpu.CompilerParams(vmem_limit_bytes=VMEM_LIMIT),
    )(*placed)


def inside(rows, low, count):
    return (rows >= low) & (rows < low + count)


def pick_body(given, trailing, keep, send, column, pivots, table, slots, block, sems):
    width = pivots.shape[0]
    rows = trailing.shape[0]
    lanes = column.shape[1]
    half = width // 2
    me = lax.axis_index("prow")
    core = lax.rem(me, 2)
    first = me * rows
    order = pltpu.make_async_copy(given, pivots, sems.at[0])
    load = pltpu.make_async_copy(trailing, block, sems.at[1])
    order.start()
    load.start()

    def top(i, _):
        for u in range(UNROLL):
            table[i * UNROLL + u] = i * UNROLL + u
        return 0

    def fill(i, _):
        for u in range(UNROLL):
            pivot = pivots[i * UNROLL + u]
            table[pivot] = pivot
        return 0

    def exchange(i, _):
        for u in range(UNROLL):
            k = i * UNROLL + u
            pivot = pivots[k]
            mine = table[k]
            slots[k] = table[pivot]
            table[pivot] = mine
        return 0

    lax.fori_loop(0, width // UNROLL, top, 0)
    order.wait()
    lax.fori_loop(0, width // UNROLL, fill, 0)
    lax.fori_loop(0, width // UNROLL, exchange, 0)
    load.wait()

    def pick(offset, target):
        def some(i, _):
            for u in range(UNROLL):
                j = i * UNROLL + u
                row = slots[offset + j]
                local = row - first
                own = (local >= 0) & (local < rows)
                index = jnp.where(own, local, jnp.where(me == 0, table[row], 0))
                target[pl.ds(j, 1), :] = block[pl.ds(index, 1), :]
                column[pl.ds(offset + j, 1), :] = jnp.full((1, lanes), row, jnp.int32)
            return 0

        lax.fori_loop(0, half // UNROLL, some, 0)

    pick((1 - core) * half, send)
    pick(core * half, keep)


def mark_body(column, mark):
    mark[...] = column[0 : mark.shape[0], :]


def join_body(mark, panel, diag, arrived, joined):
    del mark
    joined[0] = jnp.where(lax.rem(lax.axis_index("prow"), 2) == 1, arrived[...], diag[...])
    joined[1] = panel[...]


def chip_body(rows, keep, recv, column, *pieces):
    me = lax.axis_index("prow")
    chip, core = me // 2, lax.rem(me, 2)
    for d, piece in enumerate(pieces):
        part = lax.bitwise_xor(chip, d)
        ids = column[core * len(pieces) + part][:, 0:1]
        second = inside(ids, (2 * chip + 1) * rows, rows)
        piece[...] = jnp.where(second == (core == 1), keep[part], recv[part])


def owner_body(rows, count, column, *refs):
    pieces, outs = refs[:count], refs[count:]
    me = lax.axis_index("prow")
    chip, core = me // 2, lax.rem(me, 2)
    ids = column[core * count + chip][:, 0:1]
    holds = [inside(ids, lax.bitwise_xor(chip, d) * 2 * rows, 2 * rows) for d in range(count)]
    chosen = pieces[0][...]
    leaving = pieces[0][...]
    for d in range(1, count):
        value = pieces[d][...]
        chosen = jnp.where(holds[d], value, chosen)
        leaving = jnp.where(chip == d, value, leaving)
    for d in range(count):
        outs[d][...] = jnp.where(holds[d], leaving, chosen)


def share_body(rows, keep, recv, column, *refs):
    count = keep.shape[0]
    parts, (own, send) = refs[:count], refs[count:]
    me = lax.axis_index("prow")
    chip, core = me // 2, lax.rem(me, 2)
    for d in range(count):
        part = lax.bitwise_xor(chip, d)
        ids = column[core * count + part][:, 0:1]
        mine, theirs = keep[part], recv[part]
        second = inside(ids, (2 * chip + 1) * rows, rows)
        here = jnp.where(second == (core == 1), mine, theirs)
        there = jnp.where(second & (chip == 0), jnp.where(core == 0, mine, theirs), parts[d][...])
        own[part] = jnp.where(inside(ids, lax.bitwise_xor(me, 1) * rows, rows), here, there)
        send[part] = jnp.where(inside(ids, me * rows, rows), here, there)


def dot(a, b):
    return lax.dot(a, b, precision=lax.Precision.HIGHEST, preferred_element_type=F32)


def factor_body(count, mark, column, trailing, *refs):
    del mark
    panels = refs[:count]
    a_ref, sel_ref, base_ref, diag_t, lower_t = refs[count:]
    depth = panels[0].shape[1]
    width = depth * count
    rows = trailing.shape[0]
    me = lax.axis_index("prow")
    mine = lax.axis_index("pcol")
    for d in range(count):
        at = pl.ds(pl.multiple_of(lax.bitwise_xor(mine, d) * depth, depth), depth)
        diag_t[at, :] = panels[d][0]
        lower_t[at, :] = panels[d][1]
    i = lax.broadcasted_iota(jnp.int32, (width, width), 0)
    j = lax.broadcasted_iota(jnp.int32, (width, width), 1)
    full = diag_t[...]
    inverse = (i == j).astype(F32)
    size = 1
    while size < width:
        cross = (i // size + 1 == j // size) & (lax.rem(i // size, 2) == 0)
        block = jnp.where(cross, full, 0.0)
        inverse = inverse - (block if size == 1 else dot(inverse, dot(block, inverse)))
        size *= 2
    minus = -dot(inverse, lower_t[...])
    a_ref[...] = jnp.where(me == 0, inverse, minus).T
    ids = column[...].astype(F32).T[0:1, :]
    own = (me * rows + lax.broadcasted_iota(jnp.int32, (rows, width), 0)).astype(F32)
    match = (ids == own) & (me > 0)
    sel = jnp.where(match, 1.0, 0.0)
    sel_ref[...] = sel.astype(jnp.bfloat16)
    drop = (jnp.max(sel, axis=1, keepdims=True) > 0.0) | (me == 0)
    base_ref[...] = jnp.where(drop, 0.0, trailing[...])


def finish_body(rows, column, keep, send, own, recv, a_ref, sel_ref, base, out):
    half = keep.shape[0]
    me = lax.axis_index("prow")
    core = lax.rem(me, 2)

    def part(start, picked, arrived):
        at = pl.ds(pl.multiple_of(start, half), half)
        ids = column[at, 0:1]
        value = arrived[...]
        chosen = jnp.where(inside(ids, me * rows, rows), picked[...], value)
        high = value.astype(jnp.bfloat16)
        rest = value - high.astype(F32)
        middle = rest.astype(jnp.bfloat16)
        low = (rest - middle.astype(F32)).astype(jnp.bfloat16)
        sel = sel_ref[:, at]
        total = dot(a_ref[:, at], chosen)
        for term in (low, middle, high):
            total += lax.dot(sel, term, preferred_element_type=F32)
        return total

    first = part(core * half, keep, own)
    out[...] = base[...] + first + part((1 - core) * half, send, recv)


def on_device(trailing_in, panel_t, pivots):
    rows, cols = trailing_in.shape
    width = pivots.shape[0]
    half = width // 2
    devices = lax.axis_size("prow")
    chips = devices // 2
    spread = lax.axis_size("pcol")
    size = half // chips
    depth = panel_t.shape[0]
    assert rows == width and size * chips == half and depth * spread == width

    def array(*shape, dtype=F32):
        return pltpu.VMEM(shape, dtype)

    keep, send, column = call(
        pick_body,
        (array(half, cols), array(half, cols), array(width, 128, dtype=jnp.int32)),
        pivots,
        trailing_in,
        in_specs=(HBM, HBM),
        scratch=(
            pltpu.SMEM((width,), jnp.int32),
            pltpu.SMEM((rows * devices,), jnp.int32),
            pltpu.SMEM((width,), jnp.int32),
            pltpu.VMEM((rows, cols), F32),
            pltpu.SemaphoreType.DMA((2,)),
        ),
    )
    me = lax.axis_index("prow")
    diag, arrived, bit = panel_t, panel_t, devices // 2
    while bit:
        arrived = pair_exchange(diag, "prow", bit)
        if bit > 1:
            diag = jnp.where((me & bit) > 0, arrived, diag)
        bit //= 2
    (mark,) = call(mark_body, (array(8, 128, dtype=jnp.int32),), column)
    (joined,) = call(join_body, (array(2, depth, rows),), mark, panel_t, diag, arrived)
    panels = [joined] + [pair_exchange(joined, "pcol", d) for d in range(1, spread)]

    recv = pair_exchange(send, "prow", 1).reshape(chips, size, cols)
    cut = keep.reshape(chips, size, cols)
    ids = column.reshape(devices, size, 128)
    pieces = call(functools.partial(chip_body, rows), [array(size, cols)] * chips, cut, recv, ids)
    gathered = [pieces[0]] + [pair_exchange(pieces[d], "prow", 2 * d) for d in range(1, chips)]
    parts = call(
        functools.partial(owner_body, rows, chips), [array(size, cols)] * chips, ids, *gathered
    )
    parts = [parts[0]] + [pair_exchange(parts[d], "prow", 2 * d) for d in range(1, chips)]
    own, other = call(
        functools.partial(share_body, rows), [array(chips, size, cols)] * 2, cut, recv, ids, *parts
    )
    own = own.reshape(half, cols)
    arrived = pair_exchange(other, "prow", 1).reshape(half, cols)
    (mark,) = call(mark_body, (array(8, 128, dtype=jnp.int32),), column)
    a, sel, base = call(
        functools.partial(factor_body, spread),
        (array(rows, width), array(rows, width, dtype=jnp.bfloat16), array(rows, cols)),
        mark,
        column,
        trailing_in,
        *panels,
        scratch=(pltpu.VMEM((width, width), F32), pltpu.VMEM((width, rows), F32)),
    )
    (out,) = call(
        functools.partial(finish_body, rows),
        (jax.ShapeDtypeStruct((rows, cols), F32),),
        column,
        keep,
        send,
        own,
        arrived,
        a,
        sel,
        base,
    )
    return out


def solution(mesh):
    in_specs = (P("prow", "pcol"), P("pcol", "prow"), P())
    out_specs = P("prow", "pcol")

    return jax.shard_map(
        on_device, mesh=mesh, in_specs=in_specs, out_specs=out_specs, check_vma=False
    )
```

```python
import functools

import jax
import jax.numpy as jnp
from jax import lax
from jax.experimental import pallas as pl
from jax.experimental.pallas import tpu as pltpu
from jax.sharding import PartitionSpec as P

VMEM = pl.BlockSpec(memory_space=pltpu.VMEM)
HBM = pl.BlockSpec(memory_space=pltpu.HBM)
F32 = jnp.float32
UNROLL = 32
OUT_PIECES = 2
VMEM_LIMIT = 16 << 20


def pair_exchange(value, axis, bit):
    size = lax.axis_size(axis)
    return lax.ppermute(value, axis, [(i, i ^ bit) for i in range(size)])


def call(body, outs, *args, in_specs=None, out_specs=None, scratch=()):
    if in_specs is None:
        in_specs = [VMEM] * len(args)
    placed = [
        pltpu.with_memory_space_constraint(arg, spec.memory_space)
        for arg, spec in zip(args, in_specs)
    ]
    return kernel(body, outs, placed, in_specs, out_specs, scratch)


def kernel(body, outs, placed, in_specs, out_specs, scratch):
    return pl.pallas_call(
        body,
        out_shape=tuple(outs),
        in_specs=list(in_specs),
        out_specs=tuple(out_specs) if out_specs else (VMEM,) * len(outs),
        scratch_shapes=list(scratch),
        compiler_params=pltpu.CompilerParams(vmem_limit_bytes=VMEM_LIMIT),
    )(*placed)


def inside(rows, low, count):
    return (rows >= low) & (rows < low + count)


def pick_body(given, trailing, keep, send, column, pivots, table, slots, block, sems):
    width = pivots.shape[0]
    rows = trailing.shape[0]
    lanes = column.shape[1]
    half = width // 2
    me = lax.axis_index("prow")
    core = lax.rem(me, 2)
    order = pltpu.make_async_copy(given, pivots, sems.at[0])
    load = pltpu.make_async_copy(trailing, block, sems.at[1])
    order.start()
    load.start()

    def top(i, _):
        for u in range(UNROLL):
            table[i * UNROLL + u] = i * UNROLL + u
        return 0

    def fill(i, _):
        for u in range(UNROLL):
            pivot = pivots[i * UNROLL + u]
            table[pivot] = pivot
        return 0

    def exchange(i, _):
        for u in range(UNROLL):
            k = i * UNROLL + u
            pivot = pivots[k]
            mine = table[k]
            slots[k] = table[pivot]
            table[pivot] = mine
            table[k] = k
        return 0

    lax.fori_loop(0, width // UNROLL, top, 0)
    order.wait()
    lax.fori_loop(0, width // UNROLL, fill, 0)
    lax.fori_loop(0, width // UNROLL, exchange, 0)
    load.wait()

    def pick(offset, target, index):
        def some(i, _):
            for u in range(UNROLL):
                j = i * UNROLL + u
                row = slots[offset + j]
                target[pl.ds(j, 1), :] = block[pl.ds(index(row), 1), :]
                column[pl.ds(offset + j, 1), :] = jnp.full((1, lanes), row, jnp.int32)
            return 0

        lax.fori_loop(0, half // UNROLL, some, 0)

    @pl.when(me == 0)
    def _():
        pick((1 - core) * half, send, lambda row: table[row])
        pick(core * half, keep, lambda row: table[row])

    @pl.when(me != 0)
    def _():
        pick((1 - core) * half, send, lambda row: row & (rows - 1))
        pick(core * half, keep, lambda row: row & (rows - 1))


def mark_body(column, mark):
    mark[...] = column[0 : mark.shape[0], :]


def join_body(mark, panel, diag, arrived, joined):
    del mark
    joined[0] = jnp.where(lax.rem(lax.axis_index("prow"), 2) == 1, arrived[...], diag[...])
    joined[1] = panel[...]


def chip_body(rows, keep, recv, column, *pieces):
    me = lax.axis_index("prow")
    chip, core = me // 2, lax.rem(me, 2)
    for d, piece in enumerate(pieces):
        part = lax.bitwise_xor(chip, d)
        ids = column[core * len(pieces) + part][:, 0:1]
        second = inside(ids, (2 * chip + 1) * rows, rows)
        piece[...] = jnp.where(second == (core == 1), keep[part], recv[part])


def owner_body(rows, count, column, *refs):
    pieces, outs = refs[:count], refs[count:]
    me = lax.axis_index("prow")
    chip, core = me // 2, lax.rem(me, 2)
    ids = column[core * count + chip][:, 0:1]
    holds = [inside(ids, lax.bitwise_xor(chip, d) * 2 * rows, 2 * rows) for d in range(count)]
    chosen = pieces[0][...]
    leaving = pieces[0][...]
    for d in range(1, count):
        value = pieces[d][...]
        chosen = jnp.where(holds[d], value, chosen)
        leaving = jnp.where(chip == d, value, leaving)
    for d in range(count):
        outs[d][...] = jnp.where(holds[d], leaving, chosen)


def share_body(rows, keep, recv, column, *refs):
    count = keep.shape[0]
    parts, (own, send) = refs[:count], refs[count:]
    me = lax.axis_index("prow")
    chip, core = me // 2, lax.rem(me, 2)
    for d in range(count):
        part = lax.bitwise_xor(chip, d)
        ids = column[core * count + part][:, 0:1]
        mine, theirs = keep[part], recv[part]
        second = inside(ids, (2 * chip + 1) * rows, rows)
        here = jnp.where(second == (core == 1), mine, theirs)
        there = jnp.where(second & (chip == 0), jnp.where(core == 0, mine, theirs), parts[d][...])
        own[part] = jnp.where(inside(ids, lax.bitwise_xor(me, 1) * rows, rows), here, there)
        send[part] = jnp.where(inside(ids, me * rows, rows), here, there)


def dot(a, b):
    return lax.dot(a, b, precision=lax.Precision.HIGHEST, preferred_element_type=F32)


def triangle(blocks):
    width = blocks[0].shape[0]
    i = lax.broadcasted_iota(jnp.int32, (width, width), 0)
    j = lax.broadcasted_iota(jnp.int32, (width, width), 1)
    inverses = [(i == j).astype(F32)] * len(blocks)
    size = 1
    while size < width:
        span = min(4 * size, width)
        cross = (i // size < j // size) & (i // span == j // span)
        steps = [jnp.where(cross, block, 0.0) for block in blocks]
        if size > 1:
            steps = [dot(inverse, step) for inverse, step in zip(inverses, steps)]
        once = [
            inverse - (step if size == 1 else dot(step, inverse))
            for inverse, step in zip(inverses, steps)
        ]
        if span > 2 * size:
            twice = [dot(step, step) for step in steps]
            once = [part + dot(square, part) for square, part in zip(twice, once)]
        inverses = once
        size = span
    return inverses


def solve_upper(full, right):
    width = full.shape[0]
    half, part = width // 2, width // 4
    cuts = [slice(k * part, (k + 1) * part) for k in range(4)]
    small = triangle([full[cut, cut] for cut in cuts])
    large = []
    for k in (0, 2):
        corner = -dot(small[k], dot(full[cuts[k], cuts[k + 1]], small[k + 1]))
        upper = jnp.concatenate([small[k], corner], axis=1)
        lower = jnp.concatenate([jnp.zeros_like(corner), small[k + 1]], axis=1)
        large.append(jnp.concatenate([upper, lower], axis=0))
    second = dot(large[1], right[half:])
    first = dot(large[0], right[:half] - dot(full[:half, half:], second))
    return jnp.concatenate([first, second], axis=0)


def factor_body(count, mark, column, trailing, *refs):
    del mark
    panels = refs[:count]
    a_ref, sel_ref, base_ref, diag_t, lower_t = refs[count:]
    depth = panels[0].shape[1]
    width = depth * count
    rows = trailing.shape[0]
    me = lax.axis_index("prow")
    mine = lax.axis_index("pcol")
    for d in range(count):
        at = pl.ds(pl.multiple_of(lax.bitwise_xor(mine, d) * depth, depth), depth)
        diag_t[at, :] = panels[d][0]
        lower_t[at, :] = panels[d][1]
    i = lax.broadcasted_iota(jnp.int32, (width, rows), 0)
    j = lax.broadcasted_iota(jnp.int32, (width, rows), 1)
    right = jnp.where(me == 0, (i == j).astype(F32), -lower_t[...])
    a_ref[...] = solve_upper(diag_t[...], right).T
    ids = column[...].astype(F32).T[0:1, :]
    own = (me * rows + lax.broadcasted_iota(jnp.int32, (rows, width), 0)).astype(F32)
    match = (ids == own) & (me > 0)
    sel = jnp.where(match, 1.0, 0.0)
    sel_ref[...] = sel.astype(jnp.bfloat16)
    drop = (jnp.max(sel, axis=1, keepdims=True) > 0.0) | (me == 0)
    base_ref[...] = jnp.where(drop, 0.0, trailing[...])


def update(rows, start, column, picked, arrived, a_ref, sel_ref, at):
    half = picked.shape[0]
    slots = pl.ds(pl.multiple_of(start, half), half)
    ids = column[slots, 0:1]
    value = arrived[:, at]
    chosen = jnp.where(inside(ids, lax.axis_index("prow") * rows, rows), picked[:, at], value)
    high = value.astype(jnp.bfloat16)
    rest = value - high.astype(F32)
    middle = rest.astype(jnp.bfloat16)
    low = (rest - middle.astype(F32)).astype(jnp.bfloat16)
    sel = sel_ref[:, slots]
    total = dot(a_ref[:, slots], chosen)
    for term in (low, middle, high):
        total += lax.dot(sel, term, preferred_element_type=F32)
    return total


def half_body(rows, column, keep, own, a_ref, sel_ref, base, out):
    half = keep.shape[0]
    start = lax.rem(lax.axis_index("prow"), 2) * half
    out[...] = base[...] + update(rows, start, column, keep, own, a_ref, sel_ref, slice(None))


def finish_body(rows, column, send, recv, a_ref, sel_ref, partial, out, block, sems):
    half = send.shape[0]
    start = (1 - lax.rem(lax.axis_index("prow"), 2)) * half
    pieces = sems.shape[0]
    width = out.shape[1] // pieces
    copies = []
    for k in range(pieces):
        at = slice(k * width, (k + 1) * width)
        block[:, at] = partial[:, at] + update(rows, start, column, send, recv, a_ref, sel_ref, at)
        copies.append(pltpu.make_async_copy(block.at[:, at], out.at[:, at], sems.at[k]))
        copies[-1].start()
    for copy in copies:
        copy.wait()


def on_device(trailing_in, panel_t, pivots):
    rows, cols = trailing_in.shape
    width = pivots.shape[0]
    half = width // 2
    devices = lax.axis_size("prow")
    chips = devices // 2
    spread = lax.axis_size("pcol")
    size = half // chips
    depth = panel_t.shape[0]
    assert rows == width and rows & (rows - 1) == 0 and size * chips == half and depth * spread == width

    def array(*shape, dtype=F32):
        return pltpu.VMEM(shape, dtype)

    keep, send, column = call(
        pick_body,
        (array(half, cols), array(half, cols), array(width, 128, dtype=jnp.int32)),
        pivots,
        trailing_in,
        in_specs=(HBM, HBM),
        scratch=(
            pltpu.SMEM((width,), jnp.int32),
            pltpu.SMEM((rows * devices,), jnp.int32),
            pltpu.SMEM((width,), jnp.int32),
            pltpu.VMEM((rows, cols), F32),
            pltpu.SemaphoreType.DMA((2,)),
        ),
    )
    me = lax.axis_index("prow")
    diag, arrived, bit = panel_t, panel_t, devices // 2
    while bit:
        arrived = pair_exchange(diag, "prow", bit)
        if bit > 1:
            diag = jnp.where((me & bit) > 0, arrived, diag)
        bit //= 2
    (mark,) = call(mark_body, (array(8, 128, dtype=jnp.int32),), column)
    (joined,) = call(join_body, (array(2, depth, rows),), mark, panel_t, diag, arrived)
    panels = [joined] + [pair_exchange(joined, "pcol", d) for d in range(1, spread)]

    recv = pair_exchange(send, "prow", 1).reshape(chips, size, cols)
    cut = keep.reshape(chips, size, cols)
    ids = column.reshape(devices, size, 128)
    pieces = call(functools.partial(chip_body, rows), [array(size, cols)] * chips, cut, recv, ids)
    gathered = [pieces[0]] + [pair_exchange(pieces[d], "prow", 2 * d) for d in range(1, chips)]
    parts = call(
        functools.partial(owner_body, rows, chips), [array(size, cols)] * chips, ids, *gathered
    )
    parts = [parts[0]] + [pair_exchange(parts[d], "prow", 2 * d) for d in range(1, chips)]
    own, other = call(
        functools.partial(share_body, rows), [array(chips, size, cols)] * 2, cut, recv, ids, *parts
    )
    own = own.reshape(half, cols)
    arrived = pair_exchange(other, "prow", 1).reshape(half, cols)
    (mark,) = call(mark_body, (array(8, 128, dtype=jnp.int32),), column)
    a, sel, base = call(
        functools.partial(factor_body, spread),
        (array(rows, width), array(rows, width, dtype=jnp.bfloat16), array(rows, cols)),
        mark,
        column,
        trailing_in,
        *panels,
        scratch=(pltpu.VMEM((width, width), F32), pltpu.VMEM((width, rows), F32)),
    )
    (partial,) = call(
        functools.partial(half_body, rows), (array(rows, cols),), column, keep, own, a, sel, base
    )
    (out,) = call(
        functools.partial(finish_body, rows),
        (jax.ShapeDtypeStruct((rows, cols), F32),),
        column,
        send,
        arrived,
        a,
        sel,
        partial,
        out_specs=(HBM,),
        scratch=(pltpu.VMEM((rows, cols), F32), pltpu.SemaphoreType.DMA((OUT_PIECES,))),
    )
    return out


def solution(mesh):
    in_specs = (P("prow", "pcol"), P("pcol", "prow"), P())
    out_specs = P("prow", "pcol")

    return jax.shard_map(
        on_device, mesh=mesh, in_specs=in_specs, out_specs=out_specs, check_vma=False
    )
```

```python
import functools

import jax
import jax.numpy as jnp
from jax import lax
from jax.experimental import pallas as pl
from jax.experimental.pallas import tpu as pltpu
from jax.sharding import PartitionSpec as P

VMEM = pl.BlockSpec(memory_space=pltpu.VMEM)
HBM = pl.BlockSpec(memory_space=pltpu.HBM)
SMEM = pl.BlockSpec(memory_space=pltpu.SMEM)
F32 = jnp.float32
UNROLL = 32
OUT_PIECES = 2
VMEM_LIMIT = 16 << 20


def pair_exchange(value, axis, bit):
    size = lax.axis_size(axis)
    return lax.ppermute(value, axis, [(i, i ^ bit) for i in range(size)])


def call(body, outs, *args, in_specs=None, out_specs=None, scratch=()):
    if in_specs is None:
        in_specs = [VMEM] * len(args)
    placed = [
        pltpu.with_memory_space_constraint(arg, spec.memory_space)
        for arg, spec in zip(args, in_specs)
    ]
    return kernel(body, outs, placed, in_specs, out_specs, scratch)


def kernel(body, outs, placed, in_specs, out_specs, scratch):
    return pl.pallas_call(
        body,
        out_shape=tuple(outs),
        in_specs=list(in_specs),
        out_specs=tuple(out_specs) if out_specs else (VMEM,) * len(outs),
        scratch_shapes=list(scratch),
        compiler_params=pltpu.CompilerParams(vmem_limit_bytes=VMEM_LIMIT),
    )(*placed)


def inside(rows, low, count):
    return (rows >= low) & (rows < low + count)


def pivot_body(given, trailing, slots, table, block, pivots, sems):
    width = pivots.shape[0]
    load = pltpu.make_async_copy(given, pivots, sems.at[0])
    load.start()
    hold = pltpu.make_async_copy(trailing, block, sems.at[1])
    hold.start()

    def top(i, _):
        for u in range(UNROLL):
            table[i * UNROLL + u] = i * UNROLL + u
        return 0

    def fill(i, _):
        for u in range(UNROLL):
            pivot = pivots[i * UNROLL + u]
            table[pivot] = pivot
        return 0

    def exchange(i, _):
        for u in range(UNROLL):
            k = i * UNROLL + u
            pivot = pivots[k]
            mine = table[k]
            slots[k] = table[pivot]
            table[pivot] = mine
            table[k] = k
        return 0

    lax.fori_loop(0, width // UNROLL, top, 0)
    load.wait()
    lax.fori_loop(0, width // UNROLL, fill, 0)
    lax.fori_loop(0, width // UNROLL, exchange, 0)
    hold.wait()


def pick_body(slots, table, block, beside, column, *pieces):
    rows, count, size = block.shape[0], len(pieces), pieces[0].shape[0]
    lanes = column.shape[1]
    me = lax.axis_index("prow")
    chip, core = me // 2, lax.rem(me, 2)
    start = core * count * size

    def pick(index):
        for d, piece in enumerate(pieces):
            part = lax.bitwise_xor(chip, d) * size
            for u in range(size):
                row = slots[start + part + u]
                local = index(row)
                at = pl.ds(local & (rows - 1), 1)
                own = (local >= rows) == (core == 1)
                piece[pl.ds(u, 1), :] = jnp.where(own, block[at, :], beside[at, :])

    @pl.when(chip == 0)
    def _():
        pick(lambda row: jnp.where(row < 2 * rows, row, table[row]))

    @pl.when(chip != 0)
    def _():
        pick(lambda row: row & (2 * rows - 1))

    def ids(i, _):
        for u in range(UNROLL):
            j = i * UNROLL + u
            column[pl.ds(j, 1), :] = jnp.full((1, lanes), slots[start + j], jnp.int32)
        return 0

    lax.fori_loop(0, column.shape[0] // UNROLL, ids, 0)


def rest_body(slots, table, block, beside, column, theirs, tops):
    rows, half = block.shape[0], column.shape[0]
    lanes = column.shape[1]
    me = lax.axis_index("prow")
    core = lax.rem(me, 2)

    def pick(i, _):
        for u in range(UNROLL):
            j = i * UNROLL + u
            row = slots[(1 - core) * half + j]
            theirs[pl.ds(j, 1), :] = block[pl.ds(row & (rows - 1), 1), :]
            column[pl.ds(j, 1), :] = jnp.full((1, lanes), row, jnp.int32)
        return 0

    lax.fori_loop(0, half // UNROLL, pick, 0)

    def leave(source):
        def some(i, _):
            for u in range(UNROLL):
                j = i * UNROLL + u
                at = pl.ds(table[slots[core * half + j]], 1)
                tops[pl.ds(j, 1), :] = source[at, :]
            return 0

        lax.fori_loop(0, half // UNROLL, some, 0)

    @pl.when(me == 0)
    def _():
        leave(block)

    @pl.when(me == 1)
    def _():
        leave(beside)

    @pl.when(me > 1)
    def _():
        tops[...] = jnp.zeros_like(tops)


def mark_body(column, mark):
    mark[...] = column[0 : mark.shape[0], :]


def join_body(mark, panel, diag, arrived, joined):
    del mark
    joined[0] = jnp.where(lax.rem(lax.axis_index("prow"), 2) == 1, arrived[...], diag[...])
    joined[1] = panel[...]


def owner_body(rows, count, column, *refs):
    pieces, outs = refs[:count], refs[count:]
    me = lax.axis_index("prow")
    chip = me // 2
    ids = column[chip][:, 0:1]
    holds = [inside(ids, lax.bitwise_xor(chip, d) * 2 * rows, 2 * rows) for d in range(count)]
    chosen = pieces[0][...]
    leaving = pieces[0][...]
    for d in range(1, count):
        value = pieces[d][...]
        chosen = jnp.where(holds[d], value, chosen)
        leaving = jnp.where(chip == d, value, leaving)
    for d in range(count):
        outs[d][...] = jnp.where(holds[d], leaving, chosen)


def share_body(rows, tops, column, *refs):
    count = tops.shape[0]
    pieces, parts, (chosen, own, send) = refs[:count], refs[count : 2 * count], refs[2 * count :]
    me = lax.axis_index("prow")
    chip = me // 2
    for d in range(count):
        part = lax.bitwise_xor(chip, d)
        ids = column[part][:, 0:1]
        here = pieces[d][...]
        second = inside(ids, rows, rows) & (chip == 0)
        there = jnp.where(second, tops[part], parts[d][...])
        chosen[part] = jnp.where(inside(ids, chip * 2 * rows, 2 * rows), here, there)
        own[part] = there
        send[part] = jnp.where(inside(ids, me * rows, rows), here, there)


def dot(a, b):
    return lax.dot(a, b, precision=lax.Precision.HIGHEST, preferred_element_type=F32)


def triangle(blocks):
    width = blocks[0].shape[0]
    i = lax.broadcasted_iota(jnp.int32, (width, width), 0)
    j = lax.broadcasted_iota(jnp.int32, (width, width), 1)
    inverses = [(i == j).astype(F32)] * len(blocks)
    size = 1
    while size < width:
        span = min(4 * size, width)
        cross = (i // size < j // size) & (i // span == j // span)
        steps = [jnp.where(cross, block, 0.0) for block in blocks]
        if size > 1:
            steps = [dot(inverse, step) for inverse, step in zip(inverses, steps)]
        once = [
            inverse - (step if size == 1 else dot(step, inverse))
            for inverse, step in zip(inverses, steps)
        ]
        if span > 2 * size:
            twice = [dot(step, step) for step in steps]
            once = [part + dot(square, part) for square, part in zip(twice, once)]
        inverses = once
        size = span
    return inverses


def solve_upper(full, right):
    width = full.shape[0]
    half, part = width // 2, width // 4
    cuts = [slice(k * part, (k + 1) * part) for k in range(4)]
    small = triangle([full[cut, cut] for cut in cuts])
    large = []
    for k in (0, 2):
        corner = -dot(small[k], dot(full[cuts[k], cuts[k + 1]], small[k + 1]))
        upper = jnp.concatenate([small[k], corner], axis=1)
        lower = jnp.concatenate([jnp.zeros_like(corner), small[k + 1]], axis=1)
        large.append(jnp.concatenate([upper, lower], axis=0))
    second = dot(large[1], right[half:])
    first = dot(large[0], right[:half] - dot(full[:half, half:], second))
    return jnp.concatenate([first, second], axis=0)


def factor_body(count, mark, mine_ids, their_ids, trailing, *refs):
    del mark
    panels = refs[:count]
    a_ref, sel_ref, base_ref, diag_t, lower_t = refs[count:]
    depth = panels[0].shape[1]
    width = depth * count
    rows = trailing.shape[0]
    me = lax.axis_index("prow")
    mine = lax.axis_index("pcol")
    for d in range(count):
        at = pl.ds(pl.multiple_of(lax.bitwise_xor(mine, d) * depth, depth), depth)
        diag_t[at, :] = panels[d][0]
        lower_t[at, :] = panels[d][1]
    i = lax.broadcasted_iota(jnp.int32, (width, rows), 0)
    j = lax.broadcasted_iota(jnp.int32, (width, rows), 1)
    right = jnp.where(me == 0, (i == j).astype(F32), -lower_t[...])
    a_ref[...] = solve_upper(diag_t[...], right).T
    half = mine_ids.shape[0]
    ids = jnp.concatenate([ref[...].astype(F32).T[0:1, :] for ref in (mine_ids, their_ids)], axis=1)
    own = (me * rows + lax.broadcasted_iota(jnp.int32, (rows, 2 * half), 0)).astype(F32)
    match = (ids == own) & (me > 0)
    sel = jnp.where(match, 1.0, 0.0)
    sel_ref[...] = sel.astype(jnp.bfloat16)
    drop = (jnp.max(sel, axis=1, keepdims=True) > 0.0) | (me == 0)
    base_ref[...] = jnp.where(drop, 0.0, trailing[...])


def update(start, chosen, value, a_ref, sel):
    half = chosen.shape[0]
    slots = pl.ds(pl.multiple_of(start, half), half)
    high = value.astype(jnp.bfloat16)
    rest = value - high.astype(F32)
    middle = rest.astype(jnp.bfloat16)
    low = (rest - middle.astype(F32)).astype(jnp.bfloat16)
    total = dot(a_ref[:, slots], chosen)
    for term in (low, middle, high):
        total += lax.dot(sel, term, preferred_element_type=F32)
    return total


def half_body(chosen, own, a_ref, sel_ref, base, out):
    half = own.shape[0]
    start = lax.rem(lax.axis_index("prow"), 2) * half
    out[...] = base[...] + update(start, chosen[...], own[...], a_ref, sel_ref[:, :half])


def finish_body(rows, ids, theirs, recv, a_ref, sel_ref, partial, out, block, sems):
    half = recv.shape[0]
    me = lax.axis_index("prow")
    start = (1 - lax.rem(me, 2)) * half
    pieces = sems.shape[0]
    width = out.shape[1] // pieces
    mine = inside(ids[:, 0:1], me * rows, rows)
    copies = []
    for k in range(pieces):
        at = slice(k * width, (k + 1) * width)
        value = recv[:, at]
        chosen = jnp.where(mine, theirs[:, at], value)
        block[:, at] = partial[:, at] + update(start, chosen, value, a_ref, sel_ref[:, half:])
        copies.append(pltpu.make_async_copy(block.at[:, at], out.at[:, at], sems.at[k]))
        copies[-1].start()
    for copy in copies:
        copy.wait()


def on_device(trailing_in, panel_t, pivots):
    rows, cols = trailing_in.shape
    width = pivots.shape[0]
    half = width // 2
    devices = lax.axis_size("prow")
    chips = devices // 2
    spread = lax.axis_size("pcol")
    size = half // chips
    depth = panel_t.shape[0]
    assert rows == width and rows & (rows - 1) == 0 and size * chips == half and depth * spread == width

    def array(*shape, dtype=F32):
        return pltpu.VMEM(shape, dtype)

    beside = pair_exchange(trailing_in, "prow", 1)
    slots, table, block = call(
        pivot_body,
        (
            pltpu.SMEM((width,), jnp.int32),
            pltpu.SMEM((rows * devices,), jnp.int32),
            array(rows, cols),
        ),
        pivots,
        trailing_in,
        in_specs=(HBM, HBM),
        out_specs=(SMEM, SMEM, VMEM),
        scratch=(pltpu.SMEM((width,), jnp.int32), pltpu.SemaphoreType.DMA((2,))),
    )
    scalars = (SMEM, SMEM, VMEM, VMEM)
    column, *pieces = call(
        pick_body,
        [array(half, 128, dtype=jnp.int32)] + [array(size, cols)] * chips,
        slots,
        table,
        block,
        beside,
        in_specs=scalars,
    )
    others, theirs, tops = call(
        rest_body,
        (array(half, 128, dtype=jnp.int32), array(half, cols), array(half, cols)),
        slots,
        table,
        block,
        beside,
        in_specs=scalars,
    )
    ids = column.reshape(chips, size, 128)
    me = lax.axis_index("prow")
    diag, arrived, bit = panel_t, panel_t, devices // 2
    while bit:
        arrived = pair_exchange(diag, "prow", bit)
        if bit > 1:
            diag = jnp.where((me & bit) > 0, arrived, diag)
        bit //= 2
    (mark,) = call(mark_body, (array(8, 128, dtype=jnp.int32),), column)
    (joined,) = call(join_body, (array(2, depth, rows),), mark, panel_t, diag, arrived)
    panels = [joined] + [pair_exchange(joined, "pcol", d) for d in range(1, spread)]

    gathered = [pieces[0]] + [pair_exchange(pieces[d], "prow", 2 * d) for d in range(1, chips)]
    parts = call(
        functools.partial(owner_body, rows, chips), [array(size, cols)] * chips, ids, *gathered
    )
    parts = [parts[0]] + [pair_exchange(parts[d], "prow", 2 * d) for d in range(1, chips)]
    chosen, own, other = call(
        functools.partial(share_body, rows),
        [array(chips, size, cols)] * 3,
        tops.reshape(chips, size, cols),
        ids,
        *pieces,
        *parts,
    )
    chosen, own = chosen.reshape(half, cols), own.reshape(half, cols)
    arrived = pair_exchange(other, "prow", 1).reshape(half, cols)
    (mark,) = call(mark_body, (array(8, 128, dtype=jnp.int32),), column)
    a, sel, base = call(
        functools.partial(factor_body, spread),
        (array(rows, width), array(rows, width, dtype=jnp.bfloat16), array(rows, cols)),
        mark,
        column,
        others,
        block,
        *panels,
        scratch=(pltpu.VMEM((width, width), F32), pltpu.VMEM((width, rows), F32)),
    )
    (partial,) = call(half_body, (array(rows, cols),), chosen, own, a, sel, base)
    (out,) = call(
        functools.partial(finish_body, rows),
        (jax.ShapeDtypeStruct((rows, cols), F32),),
        others,
        theirs,
        arrived,
        a,
        sel,
        partial,
        out_specs=(HBM,),
        scratch=(pltpu.VMEM((rows, cols), F32), pltpu.SemaphoreType.DMA((OUT_PIECES,))),
    )
    return out


def solution(mesh):
    in_specs = (P("prow", "pcol"), P("pcol", "prow"), P())
    out_specs = P("prow", "pcol")

    return jax.shard_map(
        on_device, mesh=mesh, in_specs=in_specs, out_specs=out_specs, check_vma=False
    )
```

```python
import functools

import jax
import jax.numpy as jnp
from jax import lax
from jax.experimental import pallas as pl
from jax.experimental.pallas import tpu as pltpu
from jax.sharding import PartitionSpec as P

VMEM = pl.BlockSpec(memory_space=pltpu.VMEM)
HBM = pl.BlockSpec(memory_space=pltpu.HBM)
SMEM = pl.BlockSpec(memory_space=pltpu.SMEM)
F32 = jnp.float32
UNROLL = 32
OUT_PIECES = 1
VMEM_LIMIT = 16 << 20


def pair_exchange(value, axis, bit):
    size = lax.axis_size(axis)
    return lax.ppermute(value, axis, [(i, i ^ bit) for i in range(size)])


def call(body, outs, *args, in_specs=None, out_specs=None, scratch=()):
    if in_specs is None:
        in_specs = [VMEM] * len(args)
    placed = [
        pltpu.with_memory_space_constraint(arg, spec.memory_space)
        for arg, spec in zip(args, in_specs)
    ]
    return kernel(body, outs, placed, in_specs, out_specs, scratch)


def kernel(body, outs, placed, in_specs, out_specs, scratch):
    return pl.pallas_call(
        body,
        out_shape=tuple(outs),
        in_specs=list(in_specs),
        out_specs=tuple(out_specs) if out_specs else (VMEM,) * len(outs),
        scratch_shapes=list(scratch),
        compiler_params=pltpu.CompilerParams(vmem_limit_bytes=VMEM_LIMIT),
    )(*placed)


def inside(rows, low, count):
    return (rows >= low) & (rows < low + count)


def pivot_body(given, trailing, slots, table, block, pivots, sems):
    width = pivots.shape[0]
    load = pltpu.make_async_copy(given, pivots, sems.at[0])
    load.start()
    hold = pltpu.make_async_copy(trailing, block, sems.at[1])
    hold.start()

    def top(i, _):
        for u in range(UNROLL):
            table[i * UNROLL + u] = i * UNROLL + u
        return 0

    def fill(i, _):
        for u in range(UNROLL):
            pivot = pivots[i * UNROLL + u]
            table[pivot] = pivot
        return 0

    def exchange(i, _):
        for u in range(UNROLL):
            k = i * UNROLL + u
            pivot = pivots[k]
            mine = table[k]
            slots[k] = table[pivot]
            table[pivot] = mine
            table[k] = k
        return 0

    lax.fori_loop(0, width // UNROLL, top, 0)
    load.wait()
    lax.fori_loop(0, width // UNROLL, fill, 0)
    lax.fori_loop(0, width // UNROLL, exchange, 0)
    hold.wait()


def pick_body(slots, table, block, beside, column, *pieces):
    rows, count, size = block.shape[0], len(pieces), pieces[0].shape[0]
    lanes = column.shape[1]
    me = lax.axis_index("prow")
    chip, core = me // 2, lax.rem(me, 2)
    start = core * count * size

    def pick(index):
        for d, piece in enumerate(pieces):
            part = lax.bitwise_xor(chip, d) * size
            for u in range(size):
                row = slots[start + part + u]
                local = index(row)
                at = pl.ds(local & (rows - 1), 1)
                own = (local >= rows) == (core == 1)
                piece[pl.ds(u, 1), :] = jnp.where(own, block[at, :], beside[at, :])

    @pl.when(chip == 0)
    def _():
        pick(lambda row: jnp.where(row < 2 * rows, row, table[row]))

    @pl.when(chip != 0)
    def _():
        pick(lambda row: row & (2 * rows - 1))

    def ids(i, _):
        for u in range(UNROLL):
            j = i * UNROLL + u
            column[pl.ds(j, 1), :] = jnp.full((1, lanes), slots[start + j], jnp.int32)
        return 0

    lax.fori_loop(0, column.shape[0] // UNROLL, ids, 0)


def rest_body(slots, table, block, beside, column, theirs, tops):
    rows, half = block.shape[0], column.shape[0]
    lanes = column.shape[1]
    me = lax.axis_index("prow")
    core = lax.rem(me, 2)

    def pick(i, _):
        for u in range(UNROLL):
            j = i * UNROLL + u
            row = slots[(1 - core) * half + j]
            theirs[pl.ds(j, 1), :] = block[pl.ds(row & (rows - 1), 1), :]
            column[pl.ds(j, 1), :] = jnp.full((1, lanes), row, jnp.int32)
        return 0

    lax.fori_loop(0, half // UNROLL, pick, 0)

    def leave(source):
        def some(i, _):
            for u in range(UNROLL):
                j = i * UNROLL + u
                at = pl.ds(table[slots[core * half + j]], 1)
                tops[pl.ds(j, 1), :] = source[at, :]
            return 0

        lax.fori_loop(0, half // UNROLL, some, 0)

    @pl.when(me == 0)
    def _():
        leave(block)

    @pl.when(me == 1)
    def _():
        leave(beside)

    @pl.when(me > 1)
    def _():
        tops[...] = jnp.zeros_like(tops)


def mark_body(column, mark):
    mark[...] = column[0 : mark.shape[0], :]


def join_body(mark, panel, diag, arrived, joined):
    del mark
    joined[0] = jnp.where(lax.rem(lax.axis_index("prow"), 2) == 1, arrived[...], diag[...])
    joined[1] = panel[...]


def owner_body(rows, count, column, *refs):
    pieces, outs = refs[:count], refs[count:]
    me = lax.axis_index("prow")
    chip = me // 2
    ids = column[chip][:, 0:1]
    holds = [inside(ids, lax.bitwise_xor(chip, d) * 2 * rows, 2 * rows) for d in range(count)]
    chosen = pieces[0][...]
    leaving = pieces[0][...]
    for d in range(1, count):
        value = pieces[d][...]
        chosen = jnp.where(holds[d], value, chosen)
        leaving = jnp.where(chip == d, value, leaving)
    for d in range(count):
        outs[d][...] = jnp.where(holds[d], leaving, chosen)


def share_body(rows, tops, column, *refs):
    count = tops.shape[0]
    pieces, parts, (chosen, own, send) = refs[:count], refs[count : 2 * count], refs[2 * count :]
    me = lax.axis_index("prow")
    chip = me // 2
    for d in range(count):
        part = lax.bitwise_xor(chip, d)
        ids = column[part][:, 0:1]
        here = pieces[d][...]
        second = inside(ids, rows, rows) & (chip == 0)
        there = jnp.where(second, tops[part], parts[d][...])
        chosen[part] = jnp.where(inside(ids, chip * 2 * rows, 2 * rows), here, there)
        own[part] = there
        send[part] = jnp.where(inside(ids, me * rows, rows), here, there)


def dot(a, b):
    return lax.dot(a, b, precision=lax.Precision.HIGHEST, preferred_element_type=F32)


def triangle(blocks):
    width = blocks[0].shape[0]
    i = lax.broadcasted_iota(jnp.int32, (width, width), 0)
    j = lax.broadcasted_iota(jnp.int32, (width, width), 1)
    inverses = [(i == j).astype(F32)] * len(blocks)
    size = 1
    while size < width:
        span = min(4 * size, width)
        cross = (i // size < j // size) & (i // span == j // span)
        steps = [jnp.where(cross, block, 0.0) for block in blocks]
        if size > 1:
            steps = [dot(inverse, step) for inverse, step in zip(inverses, steps)]
        once = [
            inverse - (step if size == 1 else dot(step, inverse))
            for inverse, step in zip(inverses, steps)
        ]
        if span > 2 * size:
            twice = [dot(step, step) for step in steps]
            once = [part + dot(square, part) for square, part in zip(twice, once)]
        inverses = once
        size = span
    return inverses


def solve_upper(full, right):
    width = full.shape[0]
    half, part = width // 2, width // 4
    cuts = [slice(k * part, (k + 1) * part) for k in range(4)]
    small = triangle([full[cut, cut] for cut in cuts])
    large = []
    for k in (0, 2):
        corner = -dot(small[k], dot(full[cuts[k], cuts[k + 1]], small[k + 1]))
        upper = jnp.concatenate([small[k], corner], axis=1)
        lower = jnp.concatenate([jnp.zeros_like(corner), small[k + 1]], axis=1)
        large.append(jnp.concatenate([upper, lower], axis=0))
    second = dot(large[1], right[half:])
    first = dot(large[0], right[:half] - dot(full[:half, half:], second))
    return jnp.concatenate([first, second], axis=0)


def factor_body(count, mine_ids, their_ids, trailing, *refs):
    panels = refs[:count]
    wide_ref, fine_ref, base_ref, diag_t, lower_t, a_ref = refs[count:]
    depth = panels[0].shape[1]
    width = depth * count
    rows = trailing.shape[0]
    me = lax.axis_index("prow")
    mine = lax.axis_index("pcol")
    for d in range(count):
        at = pl.ds(pl.multiple_of(lax.bitwise_xor(mine, d) * depth, depth), depth)
        diag_t[at, :] = panels[d][0]
        lower_t[at, :] = panels[d][1]
    i = lax.broadcasted_iota(jnp.int32, (width, rows), 0)
    j = lax.broadcasted_iota(jnp.int32, (width, rows), 1)
    right = jnp.where(me == 0, (i == j).astype(F32), -lower_t[...])
    a_ref[...] = solve_upper(diag_t[...], right).T
    half = mine_ids.shape[0]
    ids = jnp.concatenate([ref[...].astype(F32).T[0:1, :] for ref in (mine_ids, their_ids)], axis=1)
    own = (me * rows + lax.broadcasted_iota(jnp.int32, (rows, 2 * half), 0)).astype(F32)
    match = (ids == own) & (me > 0)
    sel = jnp.where(match, 1.0, 0.0)
    core = lax.rem(me, 2)
    for k, held in enumerate((core, 1 - core)):
        high, middle, low = terms(a_ref[:, pl.ds(pl.multiple_of(held * half, half), half)])
        chooses = sel[:, k * half : (k + 1) * half].astype(jnp.bfloat16)
        at = slice(2 * k * half, 2 * (k + 1) * half)
        wide_ref[:, at] = jnp.concatenate([high, chooses], axis=1)
        fine_ref[:, at] = jnp.concatenate([middle, low], axis=1)
    drop = (jnp.max(sel, axis=1, keepdims=True) > 0.0) | (me == 0)
    base_ref[...] = jnp.where(drop, 0.0, trailing[...])


def terms(value):
    high = value.astype(jnp.bfloat16)
    rest = value - high.astype(F32)
    middle = rest.astype(jnp.bfloat16)
    return high, middle, (rest - middle.astype(F32)).astype(jnp.bfloat16)


def update(chosen, value, wide, fine):
    half = chosen.shape[0]
    rows = terms(chosen)
    both = [jnp.concatenate(pair, axis=0) for pair in zip(rows, terms(value))]
    low = jnp.concatenate([rows[0], rows[0]], axis=0)
    products = ((wide, both[2]), (fine[:, :half], rows[1]), (wide, both[1]), (fine, low), (wide, both[0]))
    total = 0.0
    for left, right in products:
        total += lax.dot(left, right, preferred_element_type=F32)
    return total


def half_body(chosen, own, wide, fine, base, out):
    width = 2 * own.shape[0]
    out[...] = base[...] + update(chosen[...], own[...], wide[:, :width], fine[:, :width])


def finish_body(rows, ids, theirs, recv, wide, fine, partial, out, block, sems):
    half = recv.shape[0]
    me = lax.axis_index("prow")
    pieces = sems.shape[0]
    width = out.shape[1] // pieces
    mine = inside(ids[:, 0:1], me * rows, rows)
    slots = slice(2 * half, None)
    copies = []
    for k in range(pieces):
        at = slice(k * width, (k + 1) * width)
        value = recv[:, at]
        chosen = jnp.where(mine, theirs[:, at], value)
        block[:, at] = partial[:, at] + update(chosen, value, wide[:, slots], fine[:, slots])
        copies.append(pltpu.make_async_copy(block.at[:, at], out.at[:, at], sems.at[k]))
        copies[-1].start()
    for copy in copies:
        copy.wait()


def on_device(trailing_in, panel_t, pivots):
    rows, cols = trailing_in.shape
    width = pivots.shape[0]
    half = width // 2
    devices = lax.axis_size("prow")
    chips = devices // 2
    spread = lax.axis_size("pcol")
    size = half // chips
    depth = panel_t.shape[0]
    assert rows == width and rows & (rows - 1) == 0 and size * chips == half and depth * spread == width

    def array(*shape, dtype=F32):
        return pltpu.VMEM(shape, dtype)

    beside = pair_exchange(trailing_in, "prow", 1)
    slots, table, block = call(
        pivot_body,
        (
            pltpu.SMEM((width,), jnp.int32),
            pltpu.SMEM((rows * devices,), jnp.int32),
            array(rows, cols),
        ),
        pivots,
        trailing_in,
        in_specs=(HBM, HBM),
        out_specs=(SMEM, SMEM, VMEM),
        scratch=(pltpu.SMEM((width,), jnp.int32), pltpu.SemaphoreType.DMA((2,))),
    )
    scalars = (SMEM, SMEM, VMEM, VMEM)
    column, *pieces = call(
        pick_body,
        [array(half, 128, dtype=jnp.int32)] + [array(size, cols)] * chips,
        slots,
        table,
        block,
        beside,
        in_specs=scalars,
    )
    others, theirs, tops = call(
        rest_body,
        (array(half, 128, dtype=jnp.int32), array(half, cols), array(half, cols)),
        slots,
        table,
        block,
        beside,
        in_specs=scalars,
    )
    ids = column.reshape(chips, size, 128)
    me = lax.axis_index("prow")
    diag, arrived, bit = panel_t, panel_t, devices // 2
    while bit:
        arrived = pair_exchange(diag, "prow", bit)
        if bit > 1:
            diag = jnp.where((me & bit) > 0, arrived, diag)
        bit //= 2
    (mark,) = call(mark_body, (array(8, 128, dtype=jnp.int32),), column)
    (joined,) = call(join_body, (array(2, depth, rows),), mark, panel_t, diag, arrived)
    panels = [joined] + [pair_exchange(joined, "pcol", d) for d in range(1, spread)]

    gathered = [pieces[0]] + [pair_exchange(pieces[d], "prow", 2 * d) for d in range(1, chips)]
    parts = call(
        functools.partial(owner_body, rows, chips), [array(size, cols)] * chips, ids, *gathered
    )
    parts = [parts[0]] + [pair_exchange(parts[d], "prow", 2 * d) for d in range(1, chips)]
    chosen, own, other = call(
        functools.partial(share_body, rows),
        [array(chips, size, cols)] * 3,
        tops.reshape(chips, size, cols),
        ids,
        *pieces,
        *parts,
    )
    chosen, own = chosen.reshape(half, cols), own.reshape(half, cols)
    arrived = pair_exchange(other, "prow", 1).reshape(half, cols)
    wide, fine, base = call(
        functools.partial(factor_body, spread),
        (
            array(rows, 2 * width, dtype=jnp.bfloat16),
            array(rows, 2 * width, dtype=jnp.bfloat16),
            array(rows, cols),
        ),
        column,
        others,
        block,
        *panels,
        scratch=(array(width, width), array(width, rows), array(rows, width)),
    )
    (partial,) = call(half_body, (array(rows, cols),), chosen, own, wide, fine, base)
    (out,) = call(
        functools.partial(finish_body, rows),
        (jax.ShapeDtypeStruct((rows, cols), F32),),
        others,
        theirs,
        arrived,
        wide,
        fine,
        partial,
        out_specs=(HBM,),
        scratch=(pltpu.VMEM((rows, cols), F32), pltpu.SemaphoreType.DMA((OUT_PIECES,))),
    )
    return out


def solution(mesh):
    in_specs = (P("prow", "pcol"), P("pcol", "prow"), P())
    out_specs = P("prow", "pcol")

    return jax.shard_map(
        on_device, mesh=mesh, in_specs=in_specs, out_specs=out_specs, check_vma=False
    )
```
